32 devices in a mesh: blk: 8 (over z, y), slab: 4 (over x, core).
Axes of the slice: x: 2, y: 2, z: 4, core: 2. Of those that a mesh axis runs over, the one named last changes fastest.
Arguments:
- orbitals: bfloat16 [192, 8, 8, 128], P('blk', 'slab'), may hold values from -6 to 6
- energies: bfloat16 [192], P('blk'), may hold values from -2 to -0.5
- trial_potential: float32 [8, 8, 8, 128], P('blk', 'slab'), may hold values from -6 to 6
- local_potential: float32 [8, 8, 128], P('slab'), may hold values from 0 to 1
- beta: float32 [64, 128], P('slab'), may hold values from -1.25 to 1.25
- support: int32 [64, 128], P('slab'), may hold values from 0 to 2047, as said below
- slot_atom: int32 [64], P('slab'), may hold values from 0 to 31, as said below
- dcoef: float32 [32], replicated, may hold values from 1.5 to 3
Outputs:
- response: float32 [8, 8, 8, 128], P('blk', 'slab')
The draws below stay inside these ranges and needn't reach their ends.
Inputs may be any that keep to these rules, and one draw needn't show every extreme that they name: `support`: on each slab the 16 slots' supports together list every one of its 2048 cells exactly once. `slot_atom`: atom a belongs to slab a // 8; slab k lists each atom of slab k and each atom of slab (k + 1) modulo the slab count exactly once, in an order drawn from the seed.
All inputs are finite; a program needn't handle non-finite values.
Results may differ from the reference program's by a relative error of at most 0.0003.
Values may be sent and summed in bfloat16 or wider, within the bound.
A program may use at most 64 MiB of HBM per device.

```python
import math
import jax
import jax.numpy as jnp
from jax import lax

ORB = 24
POT_DEV = 1
CZ = 2
GY = 8
GX = 128
A_DEV = 8
ITERS = 3
LOC = 16
SUP = 128
NZ = 8
NATOM = 32
NORB = 192
NPOT = 8
N_BLK = 8
N_SLAB = 4


def draw_support(key, part):
    keys = jax.random.split(key, N_SLAB)

    def one_slab(slab_key):
        return jax.random.permutation(slab_key, CZ * GY * GX)
    orders = jax.vmap(one_slab)(keys)
    return orders.reshape(N_SLAB * LOC, SUP).astype(jnp.int32)


def draw_slot_atom(key, part):
    keys = jax.random.split(key, N_SLAB)

    def one_slab(slab_key, slab):
        first, second, third = jax.random.split(slab_key, 3)
        owned = slab * A_DEV + jax.random.permutation(first, A_DEV)
        above = (slab + 1) % N_SLAB * A_DEV + jax.random.permutation(second, A_DEV)
        listed = jnp.concatenate([owned, above], 0)
        return listed[jax.random.permutation(third, 2 * A_DEV)]
    lists = jax.vmap(one_slab)(keys, jnp.arange(N_SLAB, dtype=jnp.int32))
    return lists.reshape(-1).astype(jnp.int32)


def shard_levels(key, dims, pieces, least, top_value):
    gain, own = 1.0, jax.random.fold_in(key, 6)
    for dim, shards_of in pieces:
        heights = jnp.exp(jax.random.uniform(jax.random.fold_in(own, dim), (shards_of,), jnp.float32, least / len(pieces), top_value / len(pieces)))
        gain = gain * jnp.repeat(heights, dims[dim] // shards_of).reshape([-1 if axis == dim else 1 for axis in range(len(dims))])
    return gain


def centred(rng, shape, width, limit, pieces=(), kind=jnp.bfloat16):
    drawn = width * jax.random.normal(rng, shape, jnp.float32)
    if pieces:
        drawn = drawn * shard_levels(rng, shape, pieces, -0.22, 0.18)
    return jnp.clip(drawn, -limit, limit).astype(kind)


def setup_inputs(seed: int = 0) -> dict:
    arg_keys = jax.random.split(jax.random.key(seed), 9)
    orbitals = centred(arg_keys[0], (NORB, NZ, GY, GX), 1.0, 6.0, ((0, 8), (1, 4)))
    energies = jnp.clip(-2.0 + 1.5 * jax.random.uniform(arg_keys[1], (NORB,), jnp.float32) ** shard_levels(arg_keys[1], (NORB,), ((0, 8),), -0.2, 0.2), -2.0, -0.5).astype(jnp.bfloat16)
    trial_potential = centred(arg_keys[2], (NPOT, NZ, GY, GX), 1.0, 6.0, ((0, 8), (1, 4)), jnp.float32)
    local_potential = jnp.clip(1.0 * jax.random.uniform(arg_keys[3], (NZ, GY, GX), jnp.float32) ** shard_levels(arg_keys[3], (NZ, GY, GX), ((0, 4),), -0.2, 0.2), 0.0, 1.0)
    beta = centred(arg_keys[4], (LOC * N_SLAB, SUP), (1.0 / SUP ** 0.5), 1.25, ((0, 4),), jnp.float32)
    support = draw_support(jax.random.fold_in(arg_keys[8], 71), 0)
    slot_atom = draw_slot_atom(jax.random.fold_in(arg_keys[8], 71), 0)
    dcoef = jnp.clip(jnp.exp(jax.random.uniform(arg_keys[7], (NATOM,), jnp.float32, math.log(1.5), math.log(3.0))), 1.5, 3.0)
    return dict(orbitals=orbitals, energies=energies, trial_potential=trial_potential, local_potential=local_potential, beta=beta, support=support, slot_atom=slot_atom, dcoef=dcoef)


OMEGA = 0.5


def neighbours(field):
    padded = jnp.pad(field, ((0, 0), (1, 1), (0, 0), (0, 0)))
    total = padded[:, 2:] + padded[:, :-2]
    total = total + jnp.roll(field, 1, axis=2) + jnp.roll(field, -1, axis=2)
    total = total + jnp.roll(field, 1, axis=3) + jnp.roll(field, -1, axis=3)
    return total


def reference(orbitals, energies, trial_potential, local_potential, beta, support, slot_atom, dcoef):
    cells = CZ * GY * GX
    slots = N_SLAB * LOC
    base = (jnp.arange(slots, dtype=jnp.int32) // LOC) * cells
    flat_support = (base[:, None] + support).reshape(-1).astype(jnp.int32)
    onehot = (slot_atom[:, None] == jnp.arange(NATOM, dtype=jnp.int32)[None, :]).astype(jnp.float32)

    def nonlocal_term(field):
        count = field.shape[0]
        flat = field.reshape(count, -1)
        picked = flat[:, flat_support].reshape(count, slots, SUP)
        partial_sums = jnp.sum(picked * beta, axis=-1)
        coefs = jnp.dot(partial_sums, onehot, precision=lax.Precision.HIGHEST) * dcoef
        back = jnp.dot(coefs, onehot.T, precision=lax.Precision.HIGHEST)
        values = (back[:, :, None] * beta).reshape(count, -1)
        result = jnp.zeros_like(flat).at[:, flat_support].set(values)
        return result.reshape(field.shape)

    def one_potential(index):
        holder = (index // POT_DEV).astype(jnp.int32)
        prior = ((holder + N_BLK - 1) % N_BLK).astype(jnp.int32)
        psi = jnp.concatenate([lax.dynamic_slice_in_dim(orbitals, holder * ORB, ORB, 0),
                               lax.dynamic_slice_in_dim(orbitals, prior * ORB, ORB, 0)], 0).astype(jnp.float32)
        eps = jnp.concatenate([lax.dynamic_slice_in_dim(energies, holder * ORB, ORB, 0),
                               lax.dynamic_slice_in_dim(energies, prior * ORB, ORB, 0)], 0).astype(jnp.float32)
        potential = lax.dynamic_index_in_dim(trial_potential, index, 0, keepdims=False)
        rhs = -(potential[None] * psi)
        diag = 3.0 + local_potential[None] - eps[:, None, None, None]
        state = rhs / diag
        for step in range(ITERS):
            image = diag * state - 0.5 * neighbours(state) + nonlocal_term(state)
            state = state + OMEGA * (rhs - image) / diag
        return jnp.sum(psi * state, axis=0)

    return lax.map(one_potential, jnp.arange(NPOT, dtype=jnp.int32))
```

```python
import functools

import jax
import jax.numpy as jnp
from jax import lax
from jax.experimental import pallas as pl
from jax.experimental.pallas import tpu as pltpu
from jax.sharding import PartitionSpec as P

ITERS = 3
MESH = pl.DeviceIdType.MESH


def split2(value):
    high = value.astype(jnp.bfloat16)
    low = (value - high.astype(jnp.float32)).astype(jnp.bfloat16)
    return high, low


def nt_dot(a, b):
    return lax.dot_general(a, b, (((1,), (1,)), ((), ())), preferred_element_type=jnp.float32)


def kernel(
    cfg, orb, eb, slot_atom, pot, locp, beta, support, dcoef, out,
    psi_buf, e_buf, pack, pack_buf, part, part_buf,
    psi32, psit, x0, hinv, state_a, state_b, onehot,
    psi_send, psi_recv, e_sems, pack_send, pack_recv, part_send, part_recv,
):
    n, nb, u, up, planes, gy, gx, atoms = cfg
    half = n // 2
    rows = planes * gy
    nz = n * planes
    d, k = lax.axis_index("blk"), lax.axis_index("slab")
    before = lax.rem(d + nb - 1, nb)
    after = lax.rem(d + 1, nb)

    barrier = pltpu.get_barrier_semaphore()
    for j in range(1, n):
        pl.semaphore_signal(
            barrier, inc=1, device_id=(d, lax.rem(k + j, n)), device_id_type=MESH)

    @pl.when(k >= half)
    def _():
        for j in range(n):
            pl.semaphore_signal(
                barrier, inc=1, device_id=(before, lax.rem(k + j, n)), device_id_type=MESH)

    sub_rows = lax.broadcasted_iota(jnp.int32, (rows, gx), 0)
    sub_cols = lax.broadcasted_iota(jnp.int32, (gx, gx), 0)
    acc = jnp.zeros((4 * rows, gx), jnp.float32)
    for s in range(beta.shape[0]):
        cell = support[s:s + 1, :]
        value = beta[s:s + 1, :]
        b1 = value.astype(jnp.bfloat16).astype(jnp.float32)
        b2 = (value - b1).astype(jnp.bfloat16).astype(jnp.float32)
        b3 = value - b1 - b2
        hit = sub_rows == lax.shift_right_logical(cell, 7)
        atom = jnp.full((1, 1), slot_atom[s], jnp.int32).astype(jnp.float32)
        left = jnp.concatenate(
            [jnp.where(hit, b1, 0.0), jnp.where(hit, b2, 0.0),
             jnp.where(hit, b3, 0.0), jnp.where(hit, atom, 0.0)], axis=0).astype(jnp.bfloat16)
        right = jnp.where(sub_cols == (cell & 127), 1.0, 0.0).astype(jnp.bfloat16)
        acc = acc + nt_dot(left, right)
    pack[0] = pot[...].reshape(rows, gx)
    pack[1] = locp[...].reshape(rows, gx)
    pack[2] = acc[:rows] + acc[rows:2 * rows] + acc[2 * rows:3 * rows]
    pack[3] = acc[3 * rows:]

    pl.semaphore_wait(barrier, n - 1 + half)

    def psi_copy(j):
        to = lax.rem(k + j, n)
        blk_to = lax.select(to >= half, after, d)
        return pltpu.make_async_remote_copy(
            src_ref=orb.at[lax.rem(to, half)], dst_ref=psi_buf.at[j],
            send_sem=psi_send.at[j], recv_sem=psi_recv.at[j],
            device_id=(blk_to, to), device_id_type=MESH)

    psi_local = pltpu.make_async_copy(orb.at[lax.rem(k, half)], psi_buf.at[0], psi_recv.at[0])
    e_local = pltpu.make_async_copy(eb.at[lax.rem(k, half)], e_buf, e_sems.at[1])
    e_copy = pltpu.make_async_remote_copy(
        src_ref=eb.at[lax.rem(k, half)], dst_ref=e_buf, send_sem=e_sems.at[0],
        recv_sem=e_sems.at[1], device_id=(after, k), device_id_type=MESH)

    def pack_copy(j):
        return pltpu.make_async_remote_copy(
            src_ref=pack, dst_ref=pack_buf.at[j],
            send_sem=pack_send.at[j], recv_sem=pack_recv.at[j],
            device_id=(d, lax.rem(k + j, n)), device_id_type=MESH)

    def part_copy(j):
        to = lax.rem(k + j, n)
        return pltpu.make_async_remote_copy(
            src_ref=part.at[to], dst_ref=part_buf.at[j],
            send_sem=part_send.at[j], recv_sem=part_recv.at[j],
            device_id=(d, to), device_id_type=MESH)

    @pl.when(k < half)
    def _():
        psi_local.start()
        e_local.start()

    @pl.when(k >= half)
    def _():
        e_copy.start()
        psi_copy(0).start()

    for j in range(1, n):
        psi_copy(j).start()
    for j in range(1, n):
        pack_copy(j).start()

    pack_buf[0] = pack[...]
    zero = jnp.zeros((gy, up, gx), jnp.float32)
    for ref in (state_a, state_b):
        ref[0] = zero
        ref[nz + 1] = zero
    if up > u:
        psi32[u * rows:, :] = jnp.zeros(((up - u) * rows, gx), jnp.float32)
    strength = dcoef[...]
    strength = jnp.concatenate([strength, strength], axis=1)
    atom_ids = lax.rem(lax.broadcasted_iota(jnp.int32, (2 * atoms, gx), 0), atoms).astype(jnp.float32)

    def project(z, tiles):
        pairs = [split2(tile) for tile in tiles]
        high = jnp.concatenate([p[0] for p in pairs], axis=1)
        low = jnp.concatenate([p[1] for p in pairs], axis=1)
        both = jnp.concatenate([high, low], axis=0)
        return nt_dot(both, onehot[z])

    proj = jnp.zeros((2 * up, 2 * atoms), jnp.float32)
    for j in range(n):
        if j == 0:
            @pl.when(k < half)
            def _():
                psi_local.wait()
                e_local.wait()

            @pl.when(k >= half)
            def _():
                psi_copy(0).wait_recv()
                e_copy.wait_recv()
        else:
            psi_copy(j).wait_recv()
            pack_copy(j).wait_recv()
        slab = lax.rem(k + n - j, n)
        psi32[:u * rows, :] = psi_buf[j].astype(jnp.float32).reshape(u * rows, gx)
        energy = e_buf[...]
        for p in range(planes):
            z = slab * planes + p
            scaled = []
            for y in range(gy):
                row = p * gy + y
                psi = psi32[pl.ds(row, up, stride=rows), :]
                v = pack_buf[j, 0, row:row + 1, :]
                lp = pack_buf[j, 1, row:row + 1, :]
                bv = pack_buf[j, 2, row:row + 1, :]
                at = pack_buf[j, 3, row:row + 1, :]
                inv = 1.0 / (3.0 + lp - energy)
                start = -(v * psi) * inv
                psit[z, y] = psi
                hinv[z, y] = inv
                x0[z, y] = start
                state_a[z + 1, y] = start
                onehot[z, :, y * gx:(y + 1) * gx] = jnp.where(
                    atom_ids == at, 1.0, 0.0).astype(jnp.bfloat16)
                scaled.append(start * bv)
            proj = proj + project(z, scaled)

    lanes = lax.broadcasted_iota(jnp.int32, (up, 2 * atoms), 1)
    for step in range(ITERS):
        src, dst = (state_a, state_b) if step % 2 == 0 else (state_b, state_a)
        last = step == ITERS - 1
        coefs = (proj[:up] + proj[up:]) * strength
        high = coefs.astype(jnp.bfloat16).astype(jnp.float32)
        coefs = jnp.where(lanes < atoms, high, coefs - high).astype(jnp.bfloat16)
        proj = jnp.zeros((2 * up, 2 * atoms), jnp.float32)
        for j in range(n):
            slab = lax.rem(k + n - j, n)
            for p in range(planes):
                z = slab * planes + p
                back = jnp.dot(coefs, onehot[z], preferred_element_type=jnp.float32)
                scaled, sums = [], []
                for y in range(gy):
                    row = p * gy + y
                    bv = pack_buf[j, 2, row:row + 1, :]
                    old = src[z + 1, y]
                    near = (src[z, y] + src[z + 2, y]
                            + src[z + 1, (y + 1) % gy] + src[z + 1, (y - 1) % gy]
                            + pltpu.roll(old, 1, 1) + pltpu.roll(old, gx - 1, 1))
                    change = 0.25 * near - (0.5 * bv) * back[:, y * gx:(y + 1) * gx]
                    new = 0.5 * (old + x0[z, y]) + hinv[z, y] * change
                    if last:
                        sums.append(jnp.sum(psit[z, y] * new, axis=0, keepdims=True))
                    else:
                        dst[z + 1, y] = new
                        scaled.append(new * bv)
                if last:
                    part[slab, p * gy:(p + 1) * gy, :] = jnp.concatenate(sums, axis=0)
                else:
                    proj = proj + project(z, scaled)

    for j in range(1, n):
        part_copy(j).start()
    total = part[k]
    for j in range(1, n):
        part_copy(j).wait_recv()
        total = total + part_buf[j]
    out[...] = total.reshape(out.shape)

    for j in range(1, n):
        psi_copy(j).wait_send()
        pack_copy(j).wait_send()
        part_copy(j).wait_send()

    @pl.when(k >= half)
    def _():
        psi_copy(0).wait_send()
        e_copy.wait_send()


def shards(orbitals, energies, trial_potential, local_potential, beta, support, slot_atom, dcoef):
    n, nb = lax.axis_size("slab"), lax.axis_size("blk")
    count, planes, gy, gx = orbitals.shape
    half = n // 2
    u = count // half
    up = -(-u // 16) * 16
    atoms = dcoef.shape[0]
    nz, rows = n * planes, planes * gy
    orb = orbitals.reshape(half, u, planes, gy, gx)
    eb = jnp.pad(energies.astype(jnp.float32).reshape(half, u), ((0, 0), (0, up - u)),
                 constant_values=-1.0)
    eb = jnp.broadcast_to(eb[:, :, None], (half, up, gx))
    f32, bf16 = jnp.float32, jnp.bfloat16
    vmem = pl.BlockSpec(memory_space=pltpu.VMEM)
    hbm = pl.BlockSpec(memory_space=pl.ANY)
    dma = pltpu.SemaphoreType.DMA
    return pl.pallas_call(
        functools.partial(kernel, (n, nb, u, up, planes, gy, gx, atoms)),
        out_shape=jax.ShapeDtypeStruct(trial_potential.shape, f32),
        in_specs=[hbm, vmem, pl.BlockSpec(memory_space=pltpu.SMEM), vmem, vmem, vmem, vmem, vmem],
        out_specs=vmem,
        scratch_shapes=[
            pltpu.VMEM((n, u, planes, gy, gx), bf16),
            pltpu.VMEM((up, gx), f32),
            pltpu.VMEM((4, rows, gx), f32),
            pltpu.VMEM((n, 4, rows, gx), f32),
            pltpu.VMEM((n, rows, gx), f32),
            pltpu.VMEM((n, rows, gx), f32),
            pltpu.VMEM((up * rows, gx), f32),
            pltpu.VMEM((nz, gy, up, gx), f32),
            pltpu.VMEM((nz, gy, up, gx), f32),
            pltpu.VMEM((nz, gy, up, gx), f32),
            pltpu.VMEM((nz + 2, gy, up, gx), f32),
            pltpu.VMEM((nz + 2, gy, up, gx), f32),
            pltpu.VMEM((nz, 2 * atoms, gy * gx), bf16),
            dma((n,)), dma((n,)), dma((2,)), dma((n,)), dma((n,)), dma((n,)), dma((n,)),
        ],
        compiler_params=pltpu.CompilerParams(
            collective_id=0, has_side_effects=True, vmem_limit_bytes=48 << 20),
    )(orb, eb, slot_atom, trial_potential, local_potential, beta, support, dcoef.reshape(1, atoms))


def solution(mesh):
    placed = (
        P("blk", "slab", None, None),
        P("blk"),
        P("blk", "slab", None, None),
        P("slab", None, None),
        P("slab", None),
        P("slab", None),
        P("slab"),
        P(),
    )
    return jax.shard_map(
        shards, mesh=mesh, in_specs=placed, out_specs=P("blk", "slab", None, None), check_vma=False
    )
```

```python
import functools

import jax
import jax.numpy as jnp
from jax import lax
from jax.experimental import pallas as pl
from jax.experimental.pallas import tpu as pltpu
from jax.sharding import PartitionSpec as P

ITERS = 3
MESH = pl.DeviceIdType.MESH


def split2(value):
    high = value.astype(jnp.bfloat16)
    low = (value - high.astype(jnp.float32)).astype(jnp.bfloat16)
    return high, low


def nt_dot(a, b):
    return lax.dot_general(a, b, (((1,), (1,)), ((), ())), preferred_element_type=jnp.float32)


def kernel(
    cfg, orb, eng, slot_atom_in, pot, locp, beta_in, support_in, dcoef_in, out,
    psi_buf, e_buf, slot_atom, beta, support, dcoef, pack_buf, part, part_buf,
    psi32, psit, x0, hinv, state_a, state_b, onehot,
    psi_send, psi_recv, e_sems, in_sems, pack_send, pack_recv, part_send, part_recv,
):
    n, nb, u, up, planes, gy, gx, atoms = cfg
    half = n // 2
    rows = planes * gy
    nz = n * planes
    d, k = lax.axis_index("blk"), lax.axis_index("slab")
    before = lax.rem(d + nb - 1, nb)
    after = lax.rem(d + 1, nb)

    loads = [
        pltpu.make_async_copy(src, dst, in_sems.at[i]) for i, (src, dst) in enumerate((
            (support_in, support), (beta_in, beta), (slot_atom_in, slot_atom),
            (dcoef_in, dcoef), (pot.at[0], pack_buf.at[k, 0]), (locp, pack_buf.at[k, 1])))]
    for load in loads:
        load.start()

    barrier = pltpu.get_barrier_semaphore()
    for j in range(1, n):
        pl.semaphore_signal(
            barrier, inc=1, device_id=(d, lax.rem(k + j, n)), device_id_type=MESH)

    @pl.when(k >= half)
    def _():
        for j in range(n):
            pl.semaphore_signal(
                barrier, inc=1, device_id=(before, lax.rem(k + j, n)), device_id_type=MESH)

    pl.semaphore_wait(barrier, n - 1 + half)

    def psi_copy(j):
        to = lax.rem(k + j, n)
        blk_to = lax.select(to >= half, after, d)
        return pltpu.make_async_remote_copy(
            src_ref=orb.at[lax.rem(to, half)], dst_ref=psi_buf.at[j],
            send_sem=psi_send.at[j], recv_sem=psi_recv.at[j],
            device_id=(blk_to, to), device_id_type=MESH)

    psi_local = pltpu.make_async_copy(orb.at[lax.rem(k, half)], psi_buf.at[0], psi_recv.at[0])
    e_local = pltpu.make_async_copy(eng, e_buf, e_sems.at[1])
    e_copy = pltpu.make_async_remote_copy(
        src_ref=eng, dst_ref=e_buf, send_sem=e_sems.at[0],
        recv_sem=e_sems.at[1], device_id=(after, k), device_id_type=MESH)

    def pack_copy(j):
        return pltpu.make_async_remote_copy(
            src_ref=pack_buf.at[k], dst_ref=pack_buf.at[k],
            send_sem=pack_send.at[j], recv_sem=pack_recv.at[j],
            device_id=(d, lax.rem(k + j, n)), device_id_type=MESH)

    def part_copy(j):
        to = lax.rem(k + j, n)
        return pltpu.make_async_remote_copy(
            src_ref=part.at[to], dst_ref=part_buf.at[j],
            send_sem=part_send.at[j], recv_sem=part_recv.at[j],
            device_id=(d, to), device_id_type=MESH)

    @pl.when(k < half)
    def _():
        psi_local.start()
        e_local.start()

    @pl.when(k >= half)
    def _():
        e_copy.start()
        psi_copy(0).start()

    for j in range(1, n):
        psi_copy(j).start()
    for load in loads:
        load.wait()
    sub_rows = lax.broadcasted_iota(jnp.int32, (rows, gx), 0)
    sub_cols = lax.broadcasted_iota(jnp.int32, (gx, gx), 0)
    lefts, rights = [], []
    for s in range(beta.shape[0]):
        cell = support[s:s + 1, :]
        value = beta[s:s + 1, :]
        b1 = value.astype(jnp.bfloat16).astype(jnp.float32)
        b2 = (value - b1).astype(jnp.bfloat16).astype(jnp.float32)
        b3 = value - b1 - b2
        hit = sub_rows == lax.shift_right_logical(cell, 7)
        atom = jnp.full((1, 1), slot_atom[s], jnp.int32).astype(jnp.float32)
        lefts.append(jnp.concatenate(
            [jnp.where(hit, b1, 0.0), jnp.where(hit, b2, 0.0),
             jnp.where(hit, b3, 0.0), jnp.where(hit, atom, 0.0)], axis=0).astype(jnp.bfloat16))
        rights.append(jnp.where(sub_cols == (cell & 127), 1.0, 0.0).astype(jnp.bfloat16))
    acc = nt_dot(jnp.concatenate(lefts, axis=1), jnp.concatenate(rights, axis=1))
    cellwise = acc[:rows] + acc[rows:2 * rows] + acc[2 * rows:3 * rows]
    pack_buf[k, 2] = cellwise.reshape(planes, gy, gx)
    pack_buf[k, 3] = acc[3 * rows:].reshape(planes, gy, gx)

    for j in range(1, n):
        pack_copy(j).start()

    zero = jnp.zeros((gy, up, gx), jnp.float32)
    for ref in (state_a, state_b):
        ref[0] = zero
        ref[nz + 1] = zero
    if up > u:
        psi32[u * rows:, :] = jnp.zeros(((up - u) * rows, gx), jnp.float32)
    strength = dcoef[...]
    strength = jnp.concatenate([strength, strength], axis=1)
    atom_ids = lax.rem(lax.broadcasted_iota(jnp.int32, (2 * atoms, gx), 0), atoms).astype(jnp.float32)

    def project(z, tiles):
        pairs = [split2(tile) for tile in tiles]
        high = jnp.concatenate([p[0] for p in pairs], axis=1)
        low = jnp.concatenate([p[1] for p in pairs], axis=1)
        both = jnp.concatenate([high, low], axis=0)
        return nt_dot(both, onehot[z])

    proj = jnp.zeros((2 * up, 2 * atoms), jnp.float32)
    for j in range(n):
        if j == 0:
            @pl.when(k < half)
            def _():
                psi_local.wait()
                e_local.wait()

            @pl.when(k >= half)
            def _():
                psi_copy(0).wait_recv()
                e_copy.wait_recv()
        else:
            psi_copy(j).wait_recv()
            pack_copy(j).wait_recv()
        slab = lax.rem(k + n - j, n)
        psi32[:u * rows, :] = psi_buf[j].astype(jnp.float32).reshape(u * rows, gx)
        if j == 0:
            held = e_buf[...].astype(jnp.float32).reshape(1, u * half)
            wanted = lax.broadcasted_iota(jnp.int32, (up, u * half), 0) + u * lax.rem(k, half)
            own = wanted == lax.broadcasted_iota(jnp.int32, (up, u * half), 1)
            energy = jnp.broadcast_to(
                jnp.sum(jnp.where(own, held, 0.0), axis=1, keepdims=True), (up, gx))
        for p in range(planes):
            z = slab * planes + p
            scaled = []
            for y in range(gy):
                row = p * gy + y
                psi = psi32[pl.ds(row, up, stride=rows), :]
                v = pack_buf[slab, 0, p, y:y + 1, :]
                lp = pack_buf[slab, 1, p, y:y + 1, :]
                bv = pack_buf[slab, 2, p, y:y + 1, :]
                at = pack_buf[slab, 3, p, y:y + 1, :]
                inv = 1.0 / (3.0 + lp - energy)
                start = -(v * psi) * inv
                psit[z, y] = psi
                hinv[z, y] = inv
                x0[z, y] = start
                state_a[z + 1, y] = start
                onehot[z, :, y * gx:(y + 1) * gx] = jnp.where(
                    atom_ids == at, 1.0, 0.0).astype(jnp.bfloat16)
                scaled.append(start * bv)
            proj = proj + project(z, scaled)

    lanes = lax.broadcasted_iota(jnp.int32, (up, 2 * atoms), 1)
    for step in range(ITERS):
        src, dst = (state_a, state_b) if step % 2 == 0 else (state_b, state_a)
        last = step == ITERS - 1
        coefs = (proj[:up] + proj[up:]) * strength
        high = coefs.astype(jnp.bfloat16).astype(jnp.float32)
        coefs = jnp.where(lanes < atoms, high, coefs - high).astype(jnp.bfloat16)
        proj = jnp.zeros((2 * up, 2 * atoms), jnp.float32)
        for slab in range(n):
            for p in range(planes):
                z = slab * planes + p
                back = jnp.dot(coefs, onehot[z], preferred_element_type=jnp.float32)
                scaled, sums = [], []
                for y in range(gy):
                    bv = pack_buf[slab, 2, p, y:y + 1, :]
                    old = src[z + 1, y]
                    near = (src[z, y] + src[z + 2, y]
                            + src[z + 1, (y + 1) % gy] + src[z + 1, (y - 1) % gy]
                            + pltpu.roll(old, 1, 1) + pltpu.roll(old, gx - 1, 1))
                    change = 0.25 * near - (0.5 * bv) * back[:, y * gx:(y + 1) * gx]
                    new = 0.5 * (old + x0[z, y]) + hinv[z, y] * change
                    if last:
                        sums.append(jnp.sum(psit[z, y] * new, axis=0, keepdims=True))
                    else:
                        dst[z + 1, y] = new
                        scaled.append(new * bv)
                if last:
                    part[slab, p * gy:(p + 1) * gy, :] = jnp.concatenate(sums, axis=0)
                else:
                    proj = proj + project(z, scaled)

    for j in range(1, n):
        part_copy(j).start()
    total = part[k]
    for j in range(1, n):
        part_copy(j).wait_recv()
        total = total + part_buf[j]
    out[...] = total.reshape(out.shape)

    for j in range(1, n):
        psi_copy(j).wait_send()
        pack_copy(j).wait_send()
        part_copy(j).wait_send()

    @pl.when(k >= half)
    def _():
        psi_copy(0).wait_send()
        e_copy.wait_send()


def shards(orbitals, energies, trial_potential, local_potential, beta, support, slot_atom, dcoef):
    n, nb = lax.axis_size("slab"), lax.axis_size("blk")
    count, planes, gy, gx = orbitals.shape
    half = n // 2
    u = count // half
    up = -(-u // 16) * 16
    atoms = dcoef.shape[0]
    nz, rows = n * planes, planes * gy
    orb = orbitals.reshape(half, u, planes, gy, gx)
    f32, bf16 = jnp.float32, jnp.bfloat16
    vmem = pl.BlockSpec(memory_space=pltpu.VMEM)
    hbm = pl.BlockSpec(memory_space=pltpu.HBM)
    dma = pltpu.SemaphoreType.DMA
    return pl.pallas_call(
        functools.partial(kernel, (n, nb, u, up, planes, gy, gx, atoms)),
        out_shape=jax.ShapeDtypeStruct(trial_potential.shape, f32),
        in_specs=[hbm] * 8,
        out_specs=vmem,
        scratch_shapes=[
            pltpu.VMEM((n, u, planes, gy, gx), bf16),
            pltpu.VMEM(energies.shape, bf16),
            pltpu.SMEM(slot_atom.shape, jnp.int32),
            pltpu.VMEM(beta.shape, f32),
            pltpu.VMEM(support.shape, jnp.int32),
            pltpu.VMEM((1, atoms), f32),
            pltpu.VMEM((n, 4, planes, gy, gx), f32),
            pltpu.VMEM((n, rows, gx), f32),
            pltpu.VMEM((n, rows, gx), f32),
            pltpu.VMEM((up * rows, gx), f32),
            pltpu.VMEM((nz, gy, up, gx), f32),
            pltpu.VMEM((nz, gy, up, gx), f32),
            pltpu.VMEM((nz, gy, up, gx), f32),
            pltpu.VMEM((nz + 2, gy, up, gx), f32),
            pltpu.VMEM((nz + 2, gy, up, gx), f32),
            pltpu.VMEM((nz, 2 * atoms, gy * gx), bf16),
            dma((n,)), dma((n,)), dma((2,)), dma((6,)), dma((n,)), dma((n,)), dma((n,)), dma((n,)),
        ],
        compiler_params=pltpu.CompilerParams(
            collective_id=0, has_side_effects=True, vmem_limit_bytes=60 << 20),
    )(orb, energies, slot_atom, trial_potential, local_potential, beta, support, dcoef.reshape(1, atoms))


def solution(mesh):
    placed = (
        P("blk", "slab", None, None),
        P("blk"),
        P("blk", "slab", None, None),
        P("slab", None, None),
        P("slab", None),
        P("slab", None),
        P("slab"),
        P(),
    )
    return jax.shard_map(
        shards, mesh=mesh, in_specs=placed, out_specs=P("blk", "slab", None, None), check_vma=False
    )
```

```python
import functools

import jax
import jax.numpy as jnp
from jax import lax
from jax.experimental import pallas as pl
from jax.experimental.pallas import tpu as pltpu
from jax.sharding import PartitionSpec as P

ITERS = 3
MESH = pl.DeviceIdType.MESH


def split2(value):
    high = value.astype(jnp.bfloat16)
    low = (value - high.astype(jnp.float32)).astype(jnp.bfloat16)
    return high, low


def nt_dot(a, b):
    return lax.dot_general(a, b, (((1,), (1,)), ((), ())), preferred_element_type=jnp.float32)


def kernel(
    cfg, orb, eng, slot_atom_in, pot, locp, beta_in, support_in, dcoef_in, out,
    psi_buf, e_buf, slot_atom, beta, support, dcoef, pack_buf, part, part_buf,
    psi32, psit, x0, hinv, state_a, state_b, onehot,
    psi_send, psi_recv, e_sems, in_sems, pack_send, pack_recv, part_send, part_recv,
):
    n, nb, u, up, planes, gy, gx, atoms = cfg
    half = n // 2
    rows = planes * gy
    nz = n * planes
    d, k = lax.axis_index("blk"), lax.axis_index("slab")
    takes_prior = lax.rem(k, 2) == 1
    before = lax.rem(d + nb - 1, nb)
    after = lax.rem(d + 1, nb)

    loads = [
        pltpu.make_async_copy(src, dst, in_sems.at[i]) for i, (src, dst) in enumerate((
            (support_in, support), (beta_in, beta), (slot_atom_in, slot_atom),
            (dcoef_in, dcoef), (pot.at[0], pack_buf.at[k, 0]), (locp, pack_buf.at[k, 1])))]
    for load in loads:
        load.start()

    barrier = pltpu.get_barrier_semaphore()
    for j in range(1, n):
        pl.semaphore_signal(
            barrier, inc=1, device_id=(d, lax.rem(k + j, n)), device_id_type=MESH)

    @pl.when(takes_prior)
    def _():
        for j in range(n):
            pl.semaphore_signal(
                barrier, inc=1, device_id=(before, lax.rem(k + j, n)), device_id_type=MESH)

    pl.semaphore_wait(barrier, n - 1 + half)

    def psi_copy(j):
        to = lax.rem(k + j, n)
        blk_to = lax.select(lax.rem(to, 2) == 1, after, d)
        return pltpu.make_async_remote_copy(
            src_ref=orb.at[lax.div(to, 2)], dst_ref=psi_buf.at[j],
            send_sem=psi_send.at[j], recv_sem=psi_recv.at[j],
            device_id=(blk_to, to), device_id_type=MESH)

    psi_local = pltpu.make_async_copy(orb.at[lax.div(k, 2)], psi_buf.at[0], psi_recv.at[0])
    e_local = pltpu.make_async_copy(eng, e_buf, e_sems.at[1])
    e_copy = pltpu.make_async_remote_copy(
        src_ref=eng, dst_ref=e_buf, send_sem=e_sems.at[0],
        recv_sem=e_sems.at[1], device_id=(after, k), device_id_type=MESH)

    def pack_copy(j):
        return pltpu.make_async_remote_copy(
            src_ref=pack_buf.at[k], dst_ref=pack_buf.at[k],
            send_sem=pack_send.at[j], recv_sem=pack_recv.at[j],
            device_id=(d, lax.rem(k + j, n)), device_id_type=MESH)

    def part_copy(j):
        to = lax.rem(k + j, n)
        return pltpu.make_async_remote_copy(
            src_ref=part.at[to], dst_ref=part_buf.at[j],
            send_sem=part_send.at[j], recv_sem=part_recv.at[j],
            device_id=(d, to), device_id_type=MESH)

    @pl.when(jnp.logical_not(takes_prior))
    def _():
        psi_local.start()
        e_local.start()

    @pl.when(takes_prior)
    def _():
        e_copy.start()
        psi_copy(0).start()

    for j in range(1, n):
        psi_copy(j).start()
    for load in loads:
        load.wait()
    sub_rows = lax.broadcasted_iota(jnp.int32, (rows, gx), 0)
    sub_cols = lax.broadcasted_iota(jnp.int32, (gx, gx), 0)
    lefts, rights = [], []
    for s in range(beta.shape[0]):
        cell = support[s:s + 1, :]
        value = beta[s:s + 1, :]
        b1 = value.astype(jnp.bfloat16).astype(jnp.float32)
        b2 = (value - b1).astype(jnp.bfloat16).astype(jnp.float32)
        b3 = value - b1 - b2
        hit = sub_rows == lax.shift_right_logical(cell, 7)
        atom = jnp.full((1, 1), slot_atom[s], jnp.int32).astype(jnp.float32)
        lefts.append(jnp.concatenate(
            [jnp.where(hit, b1, 0.0), jnp.where(hit, b2, 0.0),
             jnp.where(hit, b3, 0.0), jnp.where(hit, atom, 0.0)], axis=0).astype(jnp.bfloat16))
        rights.append(jnp.where(sub_cols == (cell & 127), 1.0, 0.0).astype(jnp.bfloat16))
    acc = nt_dot(jnp.concatenate(lefts, axis=1), jnp.concatenate(rights, axis=1))
    cellwise = acc[:rows] + acc[rows:2 * rows] + acc[2 * rows:3 * rows]
    pack_buf[k, 2] = cellwise.reshape(planes, gy, gx)
    pack_buf[k, 3] = acc[3 * rows:].reshape(planes, gy, gx)

    for j in range(1, n):
        pack_copy(j).start()

    zero = jnp.zeros((gy, up, gx), jnp.float32)
    for ref in (state_a, state_b):
        ref[0] = zero
        ref[nz + 1] = zero
    if up > u:
        psi32[u * rows:, :] = jnp.zeros(((up - u) * rows, gx), jnp.float32)
    strength = dcoef[...]
    strength = jnp.concatenate([strength, strength], axis=1)
    atom_ids = lax.rem(lax.broadcasted_iota(jnp.int32, (2 * atoms, gx), 0), atoms).astype(jnp.float32)

    def project(z, tiles):
        pairs = [split2(tile) for tile in tiles]
        high = jnp.concatenate([p[0] for p in pairs], axis=1)
        low = jnp.concatenate([p[1] for p in pairs], axis=1)
        both = jnp.concatenate([high, low], axis=0)
        return nt_dot(both, onehot[z])

    proj = jnp.zeros((2 * up, 2 * atoms), jnp.float32)
    for j in range(n):
        if j == 0:
            @pl.when(jnp.logical_not(takes_prior))
            def _():
                psi_local.wait()
                e_local.wait()

            @pl.when(takes_prior)
            def _():
                psi_copy(0).wait_recv()
                e_copy.wait_recv()
        else:
            psi_copy(j).wait_recv()
            pack_copy(j).wait_recv()
        slab = lax.rem(k + n - j, n)
        psi32[:u * rows, :] = psi_buf[j].astype(jnp.float32).reshape(u * rows, gx)
        if j == 0:
            held = e_buf[...].astype(jnp.float32).reshape(1, u * half)
            wanted = lax.broadcasted_iota(jnp.int32, (up, u * half), 0) + u * lax.div(k, 2)
            own = wanted == lax.broadcasted_iota(jnp.int32, (up, u * half), 1)
            energy = jnp.broadcast_to(
                jnp.sum(jnp.where(own, held, 0.0), axis=1, keepdims=True), (up, gx))
        for p in range(planes):
            z = slab * planes + p
            scaled = []
            for y in range(gy):
                row = p * gy + y
                psi = psi32[pl.ds(row, up, stride=rows), :]
                v = pack_buf[slab, 0, p, y:y + 1, :]
                lp = pack_buf[slab, 1, p, y:y + 1, :]
                bv = pack_buf[slab, 2, p, y:y + 1, :]
                at = pack_buf[slab, 3, p, y:y + 1, :]
                inv = 1.0 / (3.0 + lp - energy)
                start = -(v * psi) * inv
                psit[z, y] = psi
                hinv[z, y] = inv
                x0[z, y] = start
                state_a[z + 1, y] = start
                onehot[z, :, y * gx:(y + 1) * gx] = jnp.where(
                    atom_ids == at, 1.0, 0.0).astype(jnp.bfloat16)
                scaled.append(start * bv)
            proj = proj + project(z, scaled)

    lanes = lax.broadcasted_iota(jnp.int32, (up, 2 * atoms), 1)
    for step in range(ITERS):
        src, dst = (state_a, state_b) if step % 2 == 0 else (state_b, state_a)
        last = step == ITERS - 1
        coefs = (proj[:up] + proj[up:]) * strength
        high = coefs.astype(jnp.bfloat16).astype(jnp.float32)
        coefs = jnp.where(lanes < atoms, high, coefs - high).astype(jnp.bfloat16)
        proj = jnp.zeros((2 * up, 2 * atoms), jnp.float32)
        for j in list(range(1, n)) + [0]:
            slab = lax.rem(k + j, n) if last else j
            for p in range(planes):
                z = slab * planes + p
                back = jnp.dot(coefs, onehot[z], preferred_element_type=jnp.float32)
                scaled, sums = [], []
                for y in range(gy):
                    bv = pack_buf[slab, 2, p, y:y + 1, :]
                    old = src[z + 1, y]
                    near = (src[z, y] + src[z + 2, y]
                            + src[z + 1, (y + 1) % gy] + src[z + 1, (y - 1) % gy]
                            + pltpu.roll(old, 1, 1) + pltpu.roll(old, gx - 1, 1))
                    change = 0.25 * near - (0.5 * bv) * back[:, y * gx:(y + 1) * gx]
                    new = 0.5 * (old + x0[z, y]) + hinv[z, y] * change
                    if last:
                        sums.append(jnp.sum(psit[z, y] * new, axis=0, keepdims=True))
                    else:
                        dst[z + 1, y] = new
                        scaled.append(new * bv)
                if last:
                    part[slab, p * gy:(p + 1) * gy, :] = jnp.concatenate(sums, axis=0)
                else:
                    proj = proj + project(z, scaled)
            if last and j > 0:
                part_copy(j).start()

    total = part[k]
    for j in range(1, n):
        part_copy(j).wait_recv()
        total = total + part_buf[j]
    out[...] = total.reshape(out.shape)

    for j in range(1, n):
        psi_copy(j).wait_send()
        pack_copy(j).wait_send()
        part_copy(j).wait_send()

    @pl.when(takes_prior)
    def _():
        psi_copy(0).wait_send()
        e_copy.wait_send()


def shards(orbitals, energies, trial_potential, local_potential, beta, support, slot_atom, dcoef):
    n, nb = lax.axis_size("slab"), lax.axis_size("blk")
    count, planes, gy, gx = orbitals.shape
    half = n // 2
    u = count // half
    up = -(-u // 16) * 16
    atoms = dcoef.shape[0]
    nz, rows = n * planes, planes * gy
    orb = orbitals.reshape(half, u, planes, gy, gx)
    f32, bf16 = jnp.float32, jnp.bfloat16
    vmem = pl.BlockSpec(memory_space=pltpu.VMEM)
    hbm = pl.BlockSpec(memory_space=pltpu.HBM)
    dma = pltpu.SemaphoreType.DMA
    return pl.pallas_call(
        functools.partial(kernel, (n, nb, u, up, planes, gy, gx, atoms)),
        out_shape=jax.ShapeDtypeStruct(trial_potential.shape, f32),
        in_specs=[hbm] * 8,
        out_specs=vmem,
        scratch_shapes=[
            pltpu.VMEM((n, u, planes, gy, gx), bf16),
            pltpu.VMEM(energies.shape, bf16),
            pltpu.SMEM(slot_atom.shape, jnp.int32),
            pltpu.VMEM(beta.shape, f32),
            pltpu.VMEM(support.shape, jnp.int32),
            pltpu.VMEM((1, atoms), f32),
            pltpu.VMEM((n, 4, planes, gy, gx), f32),
            pltpu.VMEM((n, rows, gx), f32),
            pltpu.VMEM((n, rows, gx), f32),
            pltpu.VMEM((up * rows, gx), f32),
            pltpu.VMEM((nz, gy, up, gx), f32),
            pltpu.VMEM((nz, gy, up, gx), f32),
            pltpu.VMEM((nz, gy, up, gx), f32),
            pltpu.VMEM((nz + 2, gy, up, gx), f32),
            pltpu.VMEM((nz + 2, gy, up, gx), f32),
            pltpu.VMEM((nz, 2 * atoms, gy * gx), bf16),
            dma((n,)), dma((n,)), dma((2,)), dma((6,)), dma((n,)), dma((n,)), dma((n,)), dma((n,)),
        ],
        compiler_params=pltpu.CompilerParams(
            collective_id=0, has_side_effects=True, vmem_limit_bytes=32 << 20),
    )(*[pltpu.with_memory_space_constraint(a, pltpu.HBM) for a in (
        orb, energies, slot_atom, trial_potential, local_potential, beta, support,
        dcoef.reshape(1, atoms))])


def solution(mesh):
    placed = (
        P("blk", "slab", None, None),
        P("blk"),
        P("blk", "slab", None, None),
        P("slab", None, None),
        P("slab", None),
        P("slab", None),
        P("slab"),
        P(),
    )
    return jax.shard_map(
        shards, mesh=mesh, in_specs=placed, out_specs=P("blk", "slab", None, None), check_vma=False
    )
```

```python
import functools

import jax
import jax.numpy as jnp
from jax import lax
from jax.experimental import pallas as pl
from jax.experimental.pallas import tpu as pltpu
from jax.sharding import PartitionSpec as P

ITERS = 3
MESH = pl.DeviceIdType.MESH


def split2(value):
    high = value.astype(jnp.bfloat16)
    low = (value - high.astype(jnp.float32)).astype(jnp.bfloat16)
    return high, low


def nt_dot(a, b):
    return lax.dot_general(a, b, (((1,), (1,)), ((), ())), preferred_element_type=jnp.float32)


def kernel(
    cfg, orb, eng, slot_atom_in, pot, locp, beta_in, support_in, dcoef_in, out,
    psi_buf, e_buf, slot_atom, beta, support, dcoef, pack_buf, part, part_buf,
    psi32, psit, x0, hinv, state_a, state_b, onehot,
    psi_send, psi_recv, e_sems, in_sems, pack_send, pack_recv, part_send, part_recv,
):
    n, nb, u, up, planes, gy, gx, atoms = cfg
    half = n // 2
    rows = planes * gy
    nz = n * planes
    d, k = lax.axis_index("blk"), lax.axis_index("slab")
    takes_prior = lax.rem(k, 2) == 1
    before = lax.rem(d + nb - 1, nb)
    after = lax.rem(d + 1, nb)

    loads = [
        pltpu.make_async_copy(src, dst, in_sems.at[i]) for i, (src, dst) in enumerate((
            (support_in, support), (beta_in, beta), (slot_atom_in, slot_atom),
            (dcoef_in, dcoef), (pot.at[0], pack_buf.at[k, 0]), (locp, pack_buf.at[k, 1])))]
    barrier = pltpu.get_barrier_semaphore()
    for j in range(1, n):
        pl.semaphore_signal(
            barrier, inc=1, device_id=(d, lax.rem(k + j, n)), device_id_type=MESH)

    @pl.when(takes_prior)
    def _():
        for j in range(n):
            pl.semaphore_signal(
                barrier, inc=1, device_id=(before, lax.rem(k + j, n)), device_id_type=MESH)

    for load in loads:
        load.start()
    pl.semaphore_wait(barrier, n - 1 + half)

    def psi_copy(j):
        to = lax.rem(k + j, n)
        blk_to = lax.select(lax.rem(to, 2) == 1, after, d)
        return pltpu.make_async_remote_copy(
            src_ref=orb.at[lax.div(to, 2)], dst_ref=psi_buf.at[j],
            send_sem=psi_send.at[j], recv_sem=psi_recv.at[j],
            device_id=(blk_to, to), device_id_type=MESH)

    psi_local = pltpu.make_async_copy(orb.at[lax.div(k, 2)], psi_buf.at[0], psi_recv.at[0])
    e_local = pltpu.make_async_copy(eng, e_buf, e_sems.at[1])
    e_copy = pltpu.make_async_remote_copy(
        src_ref=eng, dst_ref=e_buf, send_sem=e_sems.at[0],
        recv_sem=e_sems.at[1], device_id=(after, k), device_id_type=MESH)

    def pack_copy(j):
        return pltpu.make_async_remote_copy(
            src_ref=pack_buf.at[k], dst_ref=pack_buf.at[k],
            send_sem=pack_send.at[j], recv_sem=pack_recv.at[j],
            device_id=(d, lax.rem(k + j, n)), device_id_type=MESH)

    def part_copy(j):
        to = lax.rem(k + j, n)
        return pltpu.make_async_remote_copy(
            src_ref=part.at[to], dst_ref=part_buf.at[j],
            send_sem=part_send.at[j], recv_sem=part_recv.at[j],
            device_id=(d, to), device_id_type=MESH)

    @pl.when(jnp.logical_not(takes_prior))
    def _():
        psi_local.start()
        e_local.start()

    @pl.when(takes_prior)
    def _():
        e_copy.start()
        psi_copy(0).start()

    for j in range(1, n):
        psi_copy(j).start()
    for load in loads:
        load.wait()
    sub_rows = lax.broadcasted_iota(jnp.int32, (rows, gx), 0)
    sub_cols = lax.broadcasted_iota(jnp.int32, (gx, gx), 0)
    lefts, rights = [], []
    for s in range(beta.shape[0]):
        cell = support[s:s + 1, :]
        value = beta[s:s + 1, :]
        b1 = value.astype(jnp.bfloat16).astype(jnp.float32)
        b2 = (value - b1).astype(jnp.bfloat16).astype(jnp.float32)
        b3 = value - b1 - b2
        hit = sub_rows == lax.shift_right_logical(cell, 7)
        atom = jnp.full((1, 1), slot_atom[s], jnp.int32).astype(jnp.float32)
        lefts.append(jnp.concatenate(
            [jnp.where(hit, b1, 0.0), jnp.where(hit, b2, 0.0),
             jnp.where(hit, b3, 0.0), jnp.where(hit, atom, 0.0)], axis=0).astype(jnp.bfloat16))
        rights.append(jnp.where(sub_cols == (cell & 127), 1.0, 0.0).astype(jnp.bfloat16))
    acc = nt_dot(jnp.concatenate(lefts, axis=1), jnp.concatenate(rights, axis=1))
    cellwise = acc[:rows] + acc[rows:2 * rows] + acc[2 * rows:3 * rows]
    pack_buf[k, 2] = cellwise.reshape(planes, gy, gx)
    pack_buf[k, 3] = acc[3 * rows:].reshape(planes, gy, gx)

    for j in range(1, n):
        pack_copy(j).start()

    zero = jnp.zeros((gy, up, gx), jnp.float32)
    for ref in (state_a, state_b):
        ref[0] = zero
        ref[nz + 1] = zero
    if up > u:
        psi32[u * rows:, :] = jnp.zeros(((up - u) * rows, gx), jnp.float32)
    strength = dcoef[...]
    atom_ids = lax.broadcasted_iota(jnp.int32, (atoms, gx), 0).astype(jnp.float32)

    def project(z, tiles):
        pairs = [split2(tile) for tile in tiles]
        high = jnp.concatenate([p[0] for p in pairs], axis=1)
        low = jnp.concatenate([p[1] for p in pairs], axis=1)
        both = jnp.concatenate([high, low], axis=0)
        return nt_dot(both, onehot[z, :atoms])

    proj = jnp.zeros((2 * up, atoms), jnp.float32)
    for j in range(n):
        if j == 0:
            @pl.when(jnp.logical_not(takes_prior))
            def _():
                psi_local.wait()
                e_local.wait()

            @pl.when(takes_prior)
            def _():
                psi_copy(0).wait_recv()
                e_copy.wait_recv()
        else:
            psi_copy(j).wait_recv()
            pack_copy(j).wait_recv()
        slab = lax.rem(k + n - j, n)
        psi32[:u * rows, :] = psi_buf[j].astype(jnp.float32).reshape(u * rows, gx)
        if j == 0:
            held = e_buf[...].astype(jnp.float32).reshape(1, u * half)
            wanted = lax.broadcasted_iota(jnp.int32, (up, u * half), 0) + u * lax.div(k, 2)
            own = wanted == lax.broadcasted_iota(jnp.int32, (up, u * half), 1)
            energy = jnp.broadcast_to(
                jnp.sum(jnp.where(own, held, 0.0), axis=1, keepdims=True), (up, gx))
        for p in range(planes):
            z = slab * planes + p
            scaled = []
            for y in range(gy):
                row = p * gy + y
                psi = psi32[pl.ds(row, up, stride=rows), :]
                v = pack_buf[slab, 0, p, y:y + 1, :]
                lp = pack_buf[slab, 1, p, y:y + 1, :]
                bv = pack_buf[slab, 2, p, y:y + 1, :]
                at = pack_buf[slab, 3, p, y:y + 1, :]
                inv = 1.0 / (3.0 + lp - energy)
                start = -(v * psi) * inv
                psit[z, y] = psi
                hinv[z, y] = inv
                x0[z, y] = start
                state_a[z + 1, y] = start
                hit = jnp.where(atom_ids == at, 1.0, 0.0).astype(jnp.bfloat16)
                onehot[z, :atoms, y * gx:(y + 1) * gx] = hit
                onehot[z, atoms:, y * gx:(y + 1) * gx] = hit
                scaled.append(start * bv)
            proj = proj + project(z, scaled)

    for step in range(ITERS):
        src, dst = (state_a, state_b) if step % 2 == 0 else (state_b, state_a)
        last = step == ITERS - 1
        coefs = (proj[:up] + proj[up:]) * strength
        coefs = jnp.concatenate(split2(coefs), axis=1)
        proj = jnp.zeros((2 * up, atoms), jnp.float32)
        for j in list(range(1, n)) + [0]:
            slab = lax.rem(k + j, n) if last else j
            for p in range(planes):
                z = slab * planes + p
                back = jnp.dot(coefs, onehot[z], preferred_element_type=jnp.float32)
                plane = [src[z + 1, y] for y in range(gy)]
                scaled, sums = [], []
                for y in range(gy):
                    bv = pack_buf[slab, 2, p, y:y + 1, :]
                    old = plane[y]
                    near = (src[z, y] + src[z + 2, y]
                            + plane[(y + 1) % gy] + plane[(y - 1) % gy]
                            + pltpu.roll(old, 1, 1) + pltpu.roll(old, gx - 1, 1))
                    change = 0.25 * near - (0.5 * bv) * back[:, y * gx:(y + 1) * gx]
                    new = 0.5 * (old + x0[z, y]) + hinv[z, y] * change
                    if last:
                        sums.append(jnp.sum(psit[z, y] * new, axis=0, keepdims=True))
                    else:
                        dst[z + 1, y] = new
                        scaled.append(new * bv)
                if last:
                    part[slab, p * gy:(p + 1) * gy, :] = jnp.concatenate(sums, axis=0)
                else:
                    proj = proj + project(z, scaled)
            if last and j > 0:
                part_copy(j).start()

    for j in range(1, n):
        psi_copy(j).wait_send()
        pack_copy(j).wait_send()

    @pl.when(takes_prior)
    def _():
        psi_copy(0).wait_send()
        e_copy.wait_send()

    total = part[k]
    for j in range(1, n):
        part_copy(j).wait_recv()
        total = total + part_buf[j]
    out[...] = total.reshape(out.shape)

    for j in range(1, n):
        part_copy(j).wait_send()


def shards(orbitals, energies, trial_potential, local_potential, beta, support, slot_atom, dcoef):
    n, nb = lax.axis_size("slab"), lax.axis_size("blk")
    count, planes, gy, gx = orbitals.shape
    half = n // 2
    u = count // half
    up = -(-u // 16) * 16
    atoms = dcoef.shape[0]
    nz, rows = n * planes, planes * gy
    orb = orbitals.reshape(half, u, planes, gy, gx)
    f32, bf16 = jnp.float32, jnp.bfloat16
    vmem = pl.BlockSpec(memory_space=pltpu.VMEM)
    hbm = pl.BlockSpec(memory_space=pltpu.HBM)
    dma = pltpu.SemaphoreType.DMA
    return pl.pallas_call(
        functools.partial(kernel, (n, nb, u, up, planes, gy, gx, atoms)),
        out_shape=jax.ShapeDtypeStruct(trial_potential.shape, f32),
        in_specs=[hbm] * 8,
        out_specs=vmem,
        scratch_shapes=[
            pltpu.VMEM((n, u, planes, gy, gx), bf16),
            pltpu.VMEM(energies.shape, bf16),
            pltpu.SMEM(slot_atom.shape, jnp.int32),
            pltpu.VMEM(beta.shape, f32),
            pltpu.VMEM(support.shape, jnp.int32),
            pltpu.VMEM((1, atoms), f32),
            pltpu.VMEM((n, 4, planes, gy, gx), f32),
            pltpu.VMEM((n, rows, gx), f32),
            pltpu.VMEM((n, rows, gx), f32),
            pltpu.VMEM((up * rows, gx), f32),
            pltpu.VMEM((nz, gy, up, gx), f32),
            pltpu.VMEM((nz, gy, up, gx), f32),
            pltpu.VMEM((nz, gy, up, gx), f32),
            pltpu.VMEM((nz + 2, gy, up, gx), f32),
            pltpu.VMEM((nz + 2, gy, up, gx), f32),
            pltpu.VMEM((nz, 2 * atoms, gy * gx), bf16),
            dma((n,)), dma((n,)), dma((2,)), dma((6,)), dma((n,)), dma((n,)), dma((n,)), dma((n,)),
        ],
        compiler_params=pltpu.CompilerParams(
            collective_id=0, has_side_effects=True, vmem_limit_bytes=32 << 20),
    )(*[pltpu.with_memory_space_constraint(a, pltpu.HBM) for a in (
        orb, energies, slot_atom, trial_potential, local_potential, beta, support,
        dcoef.reshape(1, atoms))])


def solution(mesh):
    placed = (
        P("blk", "slab", None, None),
        P("blk"),
        P("blk", "slab", None, None),
        P("slab", None, None),
        P("slab", None),
        P("slab", None),
        P("slab"),
        P(),
    )
    return jax.shard_map(
        shards, mesh=mesh, in_specs=placed, out_specs=P("blk", "slab", None, None), check_vma=False
    )
```
